32 devices in a mesh: dom: 16 (over z, y, x), feat: 2 (over core).
Axes of the slice: x: 2, y: 2, z: 4, core: 2. Of those that a mesh axis runs over, the one named last changes fastest.
Arguments:
- node_lat: bfloat16 [16384, 512], P('dom'), may hold values from -6 to 6
- edge_lat: bfloat16 [32768, 512], P(('dom', 'feat')), may hold values from -6 to 6
- edge_src: int32 [32768], P(('dom', 'feat')), may hold values from 0 to 1535
- edge_dst: int32 [32768], P(('dom', 'feat')), may hold values from 0 to 1023
- halo_rows: int32 [128, 64], P('dom'), may hold values from 0 to 1023
- probe_rows: int32 [256, 128], P(('dom', 'feat')), may hold values from 0 to 1023
- probe_slot: int32 [16384, 8], P(('dom', 'feat')), may hold values from 0 to 1023
- probe_wgt: float32 [16384, 8], P(('dom', 'feat')), may hold values from 0.05 to 0.3
- probe_embed: bfloat16 [16384, 512], P(('dom', 'feat')), may hold values from -6 to 6
- edge_first: bfloat16 [2, 1536, 512], replicated, may hold values from -0.15625 to 0.15625
- edge_second: bfloat16 [2, 512, 512], replicated, may hold values from -0.25 to 0.25
- node_first: bfloat16 [2, 1024, 512], replicated, may hold values from -0.1875 to 0.1875
- node_second: bfloat16 [2, 512, 512], replicated, may hold values from -0.25 to 0.25
- decode_first: bfloat16 [512, 512], replicated, may hold values from -0.25 to 0.25
- decode_second: bfloat16 [4, 512], replicated, may hold values from -0.25 to 0.25
Outputs:
- surface_out: bfloat16 [16384, 512], P('dom')
- fields: float32 [4, 16384], P(None, ('dom', 'feat'))
The draws below stay inside these ranges and needn't reach their ends.
All inputs are finite; a program needn't handle non-finite values.
Results may differ from the reference program's by a relative error of at most 0.013.
Values may be sent and summed in bfloat16 or wider, within the bound.
No kernel may reach another device: no remote copies, remote signals or barrier semaphores. Data moves between devices by JAX's collectives and lax.ppermute only.
A program may use at most 64 MiB of HBM per device.

```python
import math
import jax
import jax.numpy as jnp
import numpy as np
from jax import lax

D = 512
LAYERS = 2
NBR = 8
OUTC = 4
NEIGH = 8
SPAN = 4
NODE_DEV = 1024
EDGE_DEV = 1024
HALO_DEV = 512
REQ_DEV = 1024
PROBE_DEV = 512
HSLOT = 64
QSLOT = 128
EXT = 1536
NODES = 16384
EDGES = 32768
PROBES = 16384
N_DOM = 16
N_FEAT = 2


def touch_ends(entries, rng, smallest, largest):
    spot = [jax.random.randint(jax.random.fold_in(rng, axis), (), 0, length) for axis, length in enumerate(entries.shape)]
    longest = entries.shape.index(max(entries.shape))
    beside = spot[:longest] + [(spot[longest] + 1) % entries.shape[longest]] + spot[longest + 1:]
    return entries.at[tuple(spot)].set(smallest).at[tuple(beside)].set(largest)


def block_levels(key, extent, pieces, low, high):
    def one(position, parts):
        heights = jax.random.uniform(jax.random.fold_in(jax.random.fold_in(key, 6), position), (parts,), jnp.float32, low / len(pieces), high / len(pieces))
        return jnp.repeat(jnp.exp(heights), extent[position] // parts).reshape((-1,) + (1,) * (len(extent) - position - 1))

    level = one(*pieces[0])
    for cut in pieces[1:]:
        level = level * one(*cut)
    return level


def cumulative_ranks(amount, lean):
    weights = [(1 << 20) // math.isqrt(standing ** lean) + 1 for standing in range(1, amount + 1)]
    scale = 1 + sum(weights) // (1 << 30)
    return np.cumsum(np.array([max(1, weight // scale) for weight in weights]))


def ranked_ids(key, dims, count, lean):
    listing = cumulative_ranks(count, lean)
    ticket = jax.random.randint(jax.random.fold_in(key, 1), dims, 0, int(listing[count - 1]))
    rank = jnp.searchsorted(jnp.asarray(listing, jnp.int32), ticket, side="right")
    return jax.random.permutation(jax.random.fold_in(key, 2), count)[rank].astype(jnp.int32)


def bell_draw(rng, extent, deviation, most, shards=(), held_as=jnp.bfloat16):
    loudness = block_levels(rng, extent, shards, -0.22, 0.18) if shards else 1.0
    drawn = jax.random.normal(rng, extent, jnp.float32) * deviation * loudness
    return jnp.minimum(jnp.maximum(drawn, -most), most).astype(held_as)


def setup_inputs(seed: int = 0) -> dict:
    seeds = jax.random.split(jax.random.key(seed), 16)
    return {
        "node_lat": bell_draw(seeds[0], (NODES, D), 1.0, 6.0, ((0, 16),)),
        "edge_lat": bell_draw(seeds[1], (EDGES, D), 1.0, 6.0, ((0, 32),)),
        "edge_src": touch_ends(jax.random.randint(seeds[2], (EDGES,), 0, EXT), jax.random.fold_in(seeds[2], 1), 0, EXT - 1).astype(jnp.int32),
        "edge_dst": touch_ends(jax.random.randint(seeds[3], (EDGES,), 0, NODE_DEV), jax.random.fold_in(seeds[3], 1), 0, NODE_DEV - 1).astype(jnp.int32),
        "halo_rows": touch_ends(jax.random.randint(seeds[4], (N_DOM * NEIGH, HSLOT), 0, NODE_DEV), jax.random.fold_in(seeds[4], 1), 0, NODE_DEV - 1).astype(jnp.int32),
        "probe_rows": touch_ends(jax.random.randint(seeds[5], (N_DOM * N_FEAT * NEIGH, QSLOT), 0, NODE_DEV), jax.random.fold_in(seeds[5], 1), 0, NODE_DEV - 1).astype(jnp.int32),
        "probe_slot": touch_ends(ranked_ids(seeds[6], (PROBES, NBR), REQ_DEV, 2), jax.random.fold_in(seeds[6], 3), 0, REQ_DEV - 1).astype(jnp.int32),
        "probe_wgt": jnp.clip(0.05 + 0.25 * jax.random.uniform(seeds[7], (PROBES, NBR), jnp.float32) ** block_levels(seeds[7], (PROBES, NBR), ((0, 32),), -0.2, 0.2), 0.05, 0.3),
        "probe_embed": bell_draw(seeds[8], (PROBES, D), 1.0, 6.0, ((0, 32),)),
        "edge_first": bell_draw(seeds[9], (LAYERS, 3 * D, D), (3 * D) ** -0.5, 0.15625),
        "edge_second": bell_draw(seeds[10], (LAYERS, D, D), D ** -0.5, 0.25),
        "node_first": bell_draw(seeds[11], (LAYERS, 2 * D, D), (2 * D) ** -0.5, 0.1875),
        "node_second": bell_draw(seeds[12], (LAYERS, D, D), D ** -0.5, 0.25),
        "decode_first": bell_draw(seeds[13], (D, D), D ** -0.5, 0.25),
        "decode_second": bell_draw(seeds[14], (OUTC, D), D ** -0.5, 0.25),
    }


def layer_norm(values):
    centre = lax.optimization_barrier(jnp.mean(values, axis=-1, keepdims=True))
    shifted = values - centre
    spread = lax.optimization_barrier(jnp.mean(shifted * shifted, axis=-1, keepdims=True))
    return shifted * lax.rsqrt(spread + 1e-05)

def neighbour_offsets(width):
    return [1, -1, width, -width, width + 1, -width - 1, width - 1, 1 - width]

def one_layer(node_lat, edge_lat, edge_src, edge_dst, halo_rows, first_e, second_e, first_n, second_n):
    node_blocks = node_lat.reshape(N_DOM, NODE_DEV, D)
    send_rows = halo_rows.reshape(N_DOM, NEIGH, HSLOT)
    sent = jax.vmap(lambda source, picks: jnp.take(source, picks.reshape(-1), axis=0).reshape(NEIGH, HSLOT, D))(node_blocks, send_rows)
    offsets = neighbour_offsets(SPAN)
    halo = jnp.stack([jnp.roll(sent[:, k], offsets[k], axis=0) for k in range(NEIGH)], axis=1)
    halo = halo.reshape(N_DOM, HALO_DEV, D)
    edge_blocks = edge_lat.reshape(N_DOM, N_FEAT * EDGE_DEV, D)
    src_blocks = edge_src.reshape(N_DOM, N_FEAT * EDGE_DEV)
    dst_blocks = edge_dst.reshape(N_DOM, N_FEAT * EDGE_DEV)

    def domain(items):
        own, far, latent, senders, receivers = items
        lookup = jnp.concatenate([own, far], axis=0)
        joined = jnp.concatenate([latent, jnp.take(lookup, senders, axis=0), jnp.take(own, receivers, axis=0)], axis=1)
        hidden = jax.nn.relu(jnp.dot(joined, first_e, preferred_element_type=jnp.float32)).astype(jnp.bfloat16)
        update = jnp.dot(hidden, second_e, preferred_element_type=jnp.float32)
        new_latent = (latent.astype(jnp.float32) + layer_norm(update)).astype(jnp.bfloat16)
        summed = jax.ops.segment_sum(new_latent.astype(jnp.float32), receivers, num_segments=NODE_DEV).astype(jnp.bfloat16)
        joined_nodes = jnp.concatenate([own, summed], axis=1)
        hidden_nodes = jax.nn.relu(jnp.dot(joined_nodes, first_n, preferred_element_type=jnp.float32)).astype(jnp.bfloat16)
        update_nodes = jnp.dot(hidden_nodes, second_n, preferred_element_type=jnp.float32)
        new_own = (own.astype(jnp.float32) + layer_norm(update_nodes)).astype(jnp.bfloat16)
        return (new_own, new_latent)
    new_nodes, new_edges = lax.map(domain, (node_blocks, halo, edge_blocks, src_blocks, dst_blocks))
    return (new_nodes.reshape(NODES, D), new_edges.reshape(EDGES, D))

def reference(node_lat, edge_lat, edge_src, edge_dst, halo_rows, probe_rows, probe_slot, probe_wgt, probe_embed, edge_first, edge_second, node_first, node_second, decode_first, decode_second):
    current_nodes = node_lat
    current_edges = edge_lat
    for section_index in range(LAYERS):
        current_nodes, current_edges = one_layer(current_nodes, current_edges, edge_src, edge_dst, halo_rows, edge_first[section_index], edge_second[section_index], node_first[section_index], node_second[section_index])
    surface_out = current_nodes
    starts = (jnp.arange(N_DOM, dtype=jnp.int32) * NODE_DEV).astype(jnp.int32)
    based = probe_rows.reshape(N_DOM, N_FEAT, NEIGH, QSLOT) + starts[:, None, None, None]
    offsets = neighbour_offsets(SPAN)
    row_ids = jnp.stack([jnp.roll(based[:, :, k], offsets[k], axis=0) for k in range(NEIGH)], axis=2)
    row_ids = row_ids.reshape(N_DOM * N_FEAT, REQ_DEV).astype(jnp.int32)
    slot_blocks = probe_slot.reshape(N_DOM * N_FEAT, PROBE_DEV, NBR)
    global_ids = jax.vmap(lambda table_ids, picks: jnp.take(table_ids, picks, axis=0))(row_ids, slot_blocks)
    global_ids = global_ids.reshape(PROBES, NBR)
    interp = jnp.zeros((PROBES, D), jnp.float32)
    for slot_index in range(NBR):
        picked = jnp.take(surface_out, global_ids[:, slot_index], axis=0).astype(jnp.float32)
        interp = interp + probe_wgt[:, slot_index:slot_index + 1] * picked
    decoder_in = (interp + probe_embed.astype(jnp.float32)).astype(jnp.bfloat16)
    hidden_dec = jax.nn.relu(jnp.dot(decoder_in, decode_first, preferred_element_type=jnp.float32)).astype(jnp.bfloat16)
    fields = lax.dot_general(decode_second, hidden_dec, (((1,), (1,)), ((), ())), preferred_element_type=jnp.float32)
    return (surface_out, fields)
```

```python
import functools

import jax
import jax.numpy as jnp
from jax import lax
from jax.experimental import pallas as pl
from jax.experimental.pallas import tpu as pltpu
from jax.sharding import PartitionSpec as P

SPAN = 4
LANES = 128
CHUNK = 256
BF16 = jnp.bfloat16
F32 = jnp.float32


def steps_of_pairs(width):
    return [1, width, width + 1, width - 1]


def both_ways(value, steps):
    count = lax.axis_size("dom")
    pairs = []
    for source in range(count):
        pairs.append((2 * source, 2 * ((source + steps) % count)))
        pairs.append((2 * source + 1, 2 * ((source - steps) % count) + 1))
    return lax.ppermute(value, ("dom", "feat"), pairs)


def swapped(value):
    return lax.ppermute(value, "feat", [(0, 1), (1, 0)])


def dot(left, right):
    return jnp.dot(left, right, preferred_element_type=F32)


def normed(values):
    shifted = values - jnp.mean(values, axis=-1, keepdims=True)
    spread = jnp.mean(shifted * shifted, axis=-1, keepdims=True)
    return shifted * lax.rsqrt(spread + 1e-05)


def columns_of(row):
    return jnp.broadcast_to(row, (LANES, row.shape[1])).T


def picks(columns, base, width):
    lane = lax.broadcasted_iota(jnp.int32, columns.shape, 1)
    parts = []
    for start in range(0, width, LANES):
        parts.append(jnp.where(columns == lane + (base + start), 1.0, 0.0).astype(BF16))
    return jnp.concatenate(parts, axis=1)


def index_columns(rows_ref, first, count):
    per = rows_ref.shape[1]
    rows = [columns_of(rows_ref[pl.ds(r, 1), :]) for r in range(first // per, (first + count) // per)]
    return jnp.concatenate(rows, axis=0) if len(rows) > 1 else rows[0]


def halo_send_kernel(side_ref, rows_ref, nodes_ref, *out_refs):
    even = side_ref[0] == 0
    for i, out_ref in enumerate(out_refs):
        row = jnp.where(even, rows_ref[pl.ds(2 * i, 1), :], rows_ref[pl.ds(2 * i + 1, 1), :])
        select = picks(columns_of(row), 0, nodes_ref.shape[0])
        out_ref[...] = dot(select, nodes_ref[...]).astype(BF16)


def edge_pre_kernel(src_ref, dst_ref, nodes_ref, edges_ref, first_ref, pre_ref, own_ref, recv_ref):
    width = nodes_ref.shape[1]
    count = nodes_ref.shape[0]
    own_ref[...] = dot(nodes_ref[...], first_ref[width : 2 * width, :]).astype(BF16)
    recv_ref[...] = dot(nodes_ref[...], first_ref[2 * width : 3 * width, :]).astype(BF16)
    for start in range(0, edges_ref.shape[0], CHUNK):
        span = slice(start, start + CHUNK)
        total = dot(edges_ref[span, :], first_ref[0:width, :])
        total += dot(picks(index_columns(src_ref, start, CHUNK), 0, count), own_ref[...])
        total += dot(picks(index_columns(dst_ref, start, CHUNK), 0, count), recv_ref[...])
        pre_ref[span, :] = total


def edge_post_kernel(
    side_ref,
    src_ref,
    dst_ref,
    pre_ref,
    edges_ref,
    kept_ref,
    other_ref,
    first_ref,
    second_ref,
    new_ref,
    part_ref,
    table_ref,
    *,
    slot,
):
    side = side_ref[0]
    half = kept_ref.shape[0]
    count = part_ref.shape[0]
    total_edges = edges_ref.shape[0]
    table_ref[0:half, :] = dot(kept_ref[...], first_ref[...]).astype(BF16)
    table_ref[half : 2 * half, :] = dot(other_ref[...], first_ref[...]).astype(BF16)
    for start in range(0, total_edges, CHUNK):
        span = slice(start, start + CHUNK)
        far = index_columns(src_ref, start, CHUNK) - count
        block = far // slot
        place = (block // 2) * slot + far % slot
        place = jnp.where(block % 2 == side, place, place + half)
        place = jnp.where(far >= 0, place, -1)
        hidden = pre_ref[span, :] + dot(picks(place, 0, 2 * half), table_ref[...])
        hidden = jnp.maximum(hidden, 0.0).astype(BF16)
        update = normed(dot(hidden, second_ref[...]))
        new_ref[span, :] = (edges_ref[span, :].astype(F32) + update).astype(BF16)
    for start in range(0, count, CHUNK):
        node = lax.broadcasted_iota(jnp.int32, (CHUNK, LANES), 0) + start
        parts = []
        for r in range(total_edges // LANES):
            row = jnp.broadcast_to(dst_ref[pl.ds(r, 1), :], (CHUNK, LANES))
            parts.append(jnp.where(row == node, 1.0, 0.0).astype(BF16))
        part_ref[start : start + CHUNK, :] = dot(
            jnp.concatenate(parts, axis=1), new_ref[...]
        ).astype(BF16)


def node_rows(start, part_ref, other_ref, nodes_ref, first_ref, second_ref):
    width = nodes_ref.shape[1]
    span = slice(start, start + CHUNK)
    nodes = nodes_ref[span, :]
    summed = (part_ref[span, :].astype(F32) + other_ref[span, :].astype(F32)).astype(BF16)
    hidden = dot(nodes, first_ref[0:width, :]) + dot(summed, first_ref[width : 2 * width, :])
    hidden = jnp.maximum(hidden, 0.0).astype(BF16)
    return (nodes.astype(F32) + normed(dot(hidden, second_ref[...]))).astype(BF16)


def node_kernel(side_ref, rows_ref, part_ref, other_ref, nodes_ref, first_ref, second_ref, new_ref, *out_refs):
    for start in range(0, nodes_ref.shape[0], CHUNK):
        new_ref[start : start + CHUNK, :] = node_rows(
            start, part_ref, other_ref, nodes_ref, first_ref, second_ref
        )
    halo_send_kernel(side_ref, rows_ref, new_ref, *out_refs)


def node_probe_kernel(
    side_ref,
    rows_ref,
    far_rows_ref,
    part_ref,
    other_ref,
    nodes_ref,
    first_ref,
    second_ref,
    new_ref,
    *out_refs,
):
    even = side_ref[0] == 0
    count = nodes_ref.shape[0]
    for start in range(0, count, CHUNK):
        new_ref[start : start + CHUNK, :] = node_rows(
            start, part_ref, other_ref, nodes_ref, first_ref, second_ref
        )
    slot = rows_ref.shape[1]
    for i, out_ref in enumerate(out_refs):
        for j, lists in enumerate((rows_ref, far_rows_ref)):
            row = jnp.where(even, lists[pl.ds(2 * i, 1), :], lists[pl.ds(2 * i + 1, 1), :])
            select = picks(columns_of(row), 0, count)
            out_ref[j * slot : (j + 1) * slot, :] = dot(select, new_ref[...]).astype(BF16)


def weights_kernel(side_ref, slots_ref, wgt_ref, out_ref, *, slot):
    side = side_ref[0]
    half = out_ref.shape[1] // 2
    count = out_ref.shape[0]
    for start in range(0, count, LANES):
        lane = lax.broadcasted_iota(jnp.int32, (LANES, LANES), 1)
        places = []
        shares = []
        for k in range(slots_ref.shape[0]):
            pick = columns_of(slots_ref[pl.ds(k, 1), start : start + LANES])
            block = pick // slot
            place = (block // 2) * slot + pick % slot
            places.append(jnp.where(block % 2 == side, place, place + half))
            shares.append(columns_of(wgt_ref[pl.ds(k, 1), start : start + LANES]))
        for first in range(0, 2 * half, LANES):
            total = jnp.zeros((LANES, LANES), F32)
            for place, share in zip(places, shares):
                total += jnp.where(place == lane + first, share, 0.0)
            out_ref[start : start + LANES, first : first + LANES] = total.astype(BF16)


def decode_kernel(table_ref, embed_ref, first_ref, second_ref, a_ref, b_ref, c_ref, d_ref, other_ref, out_ref):
    slot = a_ref.shape[0] // 2
    half = 4 * slot
    interp = dot(table_ref[:, half:], other_ref[...])
    for i, ref in enumerate((a_ref, b_ref, c_ref, d_ref)):
        interp += dot(table_ref[:, i * slot : (i + 1) * slot], ref[0:slot, :])
    decoder_in = (interp + embed_ref[...].astype(F32)).astype(BF16)
    hidden = jnp.maximum(dot(decoder_in, first_ref[...]), 0.0).astype(BF16)
    out_ref[...] = lax.dot_general(
        second_ref[...], hidden, (((1,), (1,)), ((), ())), preferred_element_type=F32
    )


def whole(array):
    return pl.BlockSpec(array.shape, lambda i: (0,) * array.ndim)


def layer_rows(array, layer, block, rows):
    return pl.BlockSpec((None, rows, array.shape[2]), lambda i: (layer, block, 0))


SCALAR = pl.BlockSpec(memory_space=pltpu.SMEM)


def run(kernel, name, flops, out_shapes, in_specs, args, scratch=()):
    nbytes = sum(a.size * a.dtype.itemsize for a in args)
    return pl.pallas_call(
        kernel,
        name=name,
        grid=(1,),
        in_specs=in_specs,
        out_specs=[whole(o) for o in out_shapes],
        out_shape=out_shapes,
        scratch_shapes=list(scratch),
        cost_estimate=pl.CostEstimate(flops=flops, bytes_accessed=nbytes, transcendentals=0),
    )(*args)


def shaped(shape, dtype=BF16):
    return jax.ShapeDtypeStruct(shape, dtype)


def body(
    node_lat,
    edge_lat,
    edge_src,
    edge_dst,
    halo_rows,
    probe_rows,
    probe_slot,
    probe_wgt,
    probe_embed,
    edge_first,
    edge_second,
    node_first,
    node_second,
    decode_first,
    decode_second,
):
    steps = steps_of_pairs(SPAN)
    pairs = len(steps)
    side = lax.axis_index("feat").astype(jnp.int32).reshape(1)
    nodes, width = node_lat.shape
    edges = edge_lat.shape[0]
    slot = halo_rows.shape[1]
    qslot = probe_rows.shape[1]
    probes = probe_slot.shape[0]
    layers = edge_first.shape[0]
    src = edge_src.reshape(edges // LANES, LANES)
    dst = edge_dst.reshape(edges // LANES, LANES)
    far_rows = swapped(probe_rows)

    h = node_lat
    e = edge_lat
    sends = run(
        halo_send_kernel,
        "halo_send",
        2 * pairs * slot * nodes * width,
        [shaped((slot, width))] * pairs,
        [SCALAR, whole(halo_rows), whole(h)],
        (side, halo_rows, h),
    )
    for layer in range(layers):
        kept = [both_ways(piece, step) for piece, step in zip(sends, steps)]
        kept = jnp.concatenate(kept, axis=0)
        other = swapped(kept)
        (pre,) = run(
            edge_pre_kernel,
            f"edge_pre_{layer}",
            2 * width * width * (2 * nodes + edges) + 4 * edges * nodes * width,
            [shaped((edges, width), F32)],
            [whole(src), whole(dst), whole(h), whole(e), layer_rows(edge_first, layer, 0, 3 * width)],
            (src, dst, h, e, edge_first),
            [pltpu.VMEM((nodes, width), BF16)] * 2,
        )
        e, part = run(
            functools.partial(edge_post_kernel, slot=slot),
            f"edge_post_{layer}",
            2 * width * (2 * pairs * slot * (width + edges) + edges * (width + nodes)),
            [shaped((edges, width)), shaped((nodes, width))],
            [SCALAR, whole(src), whole(dst), whole(pre), whole(e), whole(kept), whole(other)]
            + [layer_rows(edge_first, layer, 1, width), layer_rows(edge_second, layer, 0, width)],
            (side, src, dst, pre, e, kept, other, edge_first, edge_second),
            [pltpu.VMEM((2 * pairs * slot, width), BF16)],
        )
        part_other = swapped(part)
        node_specs = [whole(part), whole(part_other), whole(h)]
        node_specs += [layer_rows(node_first, layer, 0, 2 * width), layer_rows(node_second, layer, 0, width)]
        node_args = (part, part_other, h, node_first, node_second)
        node_flops = 6 * nodes * width * width
        if layer + 1 < layers:
            h, *sends = run(
                node_kernel,
                f"node_{layer}",
                node_flops + 2 * pairs * slot * nodes * width,
                [shaped((nodes, width))] + [shaped((slot, width))] * pairs,
                [SCALAR, whole(halo_rows)] + node_specs,
                (side, halo_rows) + node_args,
            )
        else:
            h, *sends = run(
                node_probe_kernel,
                f"node_{layer}",
                node_flops + 4 * pairs * qslot * nodes * width,
                [shaped((nodes, width))] + [shaped((2 * qslot, width))] * pairs,
                [SCALAR, whole(probe_rows), whole(far_rows)] + node_specs,
                (side, probe_rows, far_rows) + node_args,
            )
    slots_t = probe_slot.T
    wgt_t = probe_wgt.T
    (table,) = run(
        functools.partial(weights_kernel, slot=qslot),
        "weights",
        8 * probes * pairs * 2 * qslot * pairs * 2,
        [shaped((probes, 2 * pairs * qslot))],
        [SCALAR, whole(slots_t), whole(wgt_t)],
        (side, slots_t, wgt_t),
    )
    got = [both_ways(piece, step) for piece, step in zip(sends, steps)]
    other = swapped(jnp.concatenate([piece[qslot:] for piece in got], axis=0))
    (fields,) = run(
        decode_kernel,
        "decode",
        2 * probes * width * (2 * pairs * qslot + width),
        [shaped((decode_second.shape[0], probes), F32)],
        [whole(a) for a in (table, probe_embed, decode_first, decode_second, *got, other)],
        (table, probe_embed, decode_first, decode_second, *got, other),
    )
    return (h, fields)


def solution(mesh):
    return jax.shard_map(
        body,
        mesh=mesh,
        in_specs=(
            P("dom", None),
            P(("dom", "feat"), None),
            P(("dom", "feat")),
            P(("dom", "feat")),
            P("dom", None),
            P(("dom", "feat"), None),
            P(("dom", "feat"), None),
            P(("dom", "feat"), None),
            P(("dom", "feat"), None),
            P(),
            P(),
            P(),
            P(),
            P(),
            P(),
        ),
        out_specs=(P("dom", None), P(None, ("dom", "feat"))),
        check_vma=False,
    )
```

```python
import functools

import jax
import jax.numpy as jnp
from jax import lax
from jax.experimental import pallas as pl
from jax.experimental.pallas import tpu as pltpu
from jax.sharding import PartitionSpec as P

SPAN = 4
LANES = 128
CHUNK = 256
VMEM_GRANT = 24 << 20
BF16 = jnp.bfloat16
F32 = jnp.float32


def steps_of_pairs(width):
    return [1, width, width + 1, width - 1]


def both_ways(value, steps):
    count = lax.axis_size("dom")
    pairs = []
    for source in range(count):
        pairs.append((2 * source, 2 * ((source + steps) % count)))
        pairs.append((2 * source + 1, 2 * ((source - steps) % count) + 1))
    return lax.ppermute(value, ("dom", "feat"), pairs)


def swapped(value):
    return lax.ppermute(value, "feat", [(0, 1), (1, 0)])


def dot(left, right):
    return jnp.dot(left, right, preferred_element_type=F32)


def normed(values):
    shifted = values - jnp.mean(values, axis=-1, keepdims=True)
    spread = jnp.mean(shifted * shifted, axis=-1, keepdims=True)
    return shifted * lax.rsqrt(spread + 1e-05)


def columns_of(row):
    return jnp.broadcast_to(row, (LANES, row.shape[1])).T


def picks(columns, base, width):
    lane = lax.broadcasted_iota(jnp.int32, columns.shape, 1)
    parts = []
    for start in range(0, width, LANES):
        parts.append(jnp.where(columns == lane + (base + start), 1.0, 0.0).astype(BF16))
    return jnp.concatenate(parts, axis=1)


def index_columns(rows_ref, first, count):
    per = rows_ref.shape[1]
    rows = [columns_of(rows_ref[pl.ds(r, 1), :]) for r in range(first // per, (first + count) // per)]
    return jnp.concatenate(rows, axis=0) if len(rows) > 1 else rows[0]


def send_rows(side, lists_ref, first, table_ref, out_ref, at):
    row = jnp.where(side == 0, lists_ref[pl.ds(first, 1), :], lists_ref[pl.ds(first + 1, 1), :])
    select = picks(columns_of(row), 0, table_ref.shape[0])
    out_ref[at : at + row.shape[1], :] = dot(select, table_ref[...]).astype(BF16)


def halo_send_kernel(side_ref, rows_ref, nodes_ref, *out_refs):
    for i, out_ref in enumerate(out_refs):
        send_rows(side_ref[0], rows_ref, 2 * i, nodes_ref, out_ref, 0)


def edge_near_kernel(src_ref, dst_ref, nodes_ref, first_ref, near_ref, recv_ref, own_ref, *, layer):
    count, width = nodes_ref.shape
    own_ref[...] = dot(nodes_ref[...], first_ref[layer, width : 2 * width, :]).astype(BF16)
    recv_ref[...] = dot(nodes_ref[...], first_ref[layer, 2 * width : 3 * width, :]).astype(BF16)
    total_edges = near_ref.shape[0]
    for start in range(0, total_edges, CHUNK):
        total = dot(picks(index_columns(src_ref, start, CHUNK), 0, count), own_ref[...])
        if start < total_edges // 2:
            total += dot(picks(index_columns(dst_ref, start, CHUNK), 0, count), recv_ref[...])
        near_ref[start : start + CHUNK, :] = total


def halo_places(far, slot, side):
    block = far // slot
    place = (block // 2) * slot + far % slot
    kept = block % 2 == side
    inside = far >= 0
    mine = jnp.where(jnp.logical_and(inside, kept), place, -1)
    others = jnp.where(jnp.logical_and(inside, jnp.logical_not(kept)), place, -1)
    return mine, others


def edge_kept_kernel(
    side_ref, src_ref, dst_ref, edges_ref, recv_ref, kept_ref, first_ref, mid_ref, table_ref, *, layer, slot
):
    side = side_ref[0]
    half, width = kept_ref.shape
    count = recv_ref.shape[0]
    total_edges = edges_ref.shape[0]
    table_ref[...] = dot(kept_ref[...], first_ref[layer, width : 2 * width, :]).astype(BF16)
    for start in range(0, total_edges, CHUNK):
        span = slice(start, start + CHUNK)
        far = index_columns(src_ref, start, CHUNK) - count
        mine, _ = halo_places(far, slot, side)
        total = dot(edges_ref[span, :], first_ref[layer, 0:width, :])
        total += dot(picks(mine, 0, half), table_ref[...])
        if start >= total_edges // 2:
            total += dot(picks(index_columns(dst_ref, start, CHUNK), 0, count), recv_ref[...])
        mid_ref[span, :] = total


def edge_post_kernel(
    side_ref,
    src_ref,
    dst_ref,
    near_ref,
    mid_ref,
    edges_ref,
    other_ref,
    first_ref,
    second_ref,
    new_ref,
    part_ref,
    table_ref,
    *,
    layer,
    slot,
):
    side = side_ref[0]
    half, width = other_ref.shape
    count = part_ref.shape[0]
    total_edges = edges_ref.shape[0]
    table_ref[...] = dot(other_ref[...], first_ref[layer, width : 2 * width, :]).astype(BF16)
    for start in range(0, total_edges, CHUNK):
        span = slice(start, start + CHUNK)
        far = index_columns(src_ref, start, CHUNK) - count
        _, others = halo_places(far, slot, side)
        hidden = near_ref[span, :] + mid_ref[span, :] + dot(picks(others, 0, half), table_ref[...])
        hidden = jnp.maximum(hidden, 0.0).astype(BF16)
        update = normed(dot(hidden, second_ref[layer]))
        new_ref[span, :] = (edges_ref[span, :].astype(F32) + update).astype(BF16)
    for start in range(0, count, CHUNK):
        node = lax.broadcasted_iota(jnp.int32, (CHUNK, LANES), 0) + start
        parts = []
        for r in range(total_edges // LANES):
            row = jnp.broadcast_to(dst_ref[pl.ds(r, 1), :], (CHUNK, LANES))
            parts.append(jnp.where(row == node, 1.0, 0.0).astype(BF16))
        part_ref[start : start + CHUNK, :] = dot(
            jnp.concatenate(parts, axis=1), new_ref[...]
        ).astype(BF16)


def node_own_kernel(nodes_ref, first_ref, own_ref, *, layer):
    own_ref[...] = dot(nodes_ref[...], first_ref[layer, 0 : nodes_ref.shape[1], :])


def node_rows(layer, own_ref, part_ref, other_ref, nodes_ref, first_ref, second_ref, new_ref):
    count, width = nodes_ref.shape
    for start in range(0, count, CHUNK):
        span = slice(start, start + CHUNK)
        summed = (part_ref[span, :].astype(F32) + other_ref[span, :].astype(F32)).astype(BF16)
        hidden = own_ref[span, :] + dot(summed, first_ref[layer, width : 2 * width, :])
        hidden = jnp.maximum(hidden, 0.0).astype(BF16)
        update = normed(dot(hidden, second_ref[layer]))
        new_ref[span, :] = (nodes_ref[span, :].astype(F32) + update).astype(BF16)


def node_kernel(
    side_ref, rows_ref, own_ref, part_ref, other_ref, nodes_ref, first_ref, second_ref, new_ref, *out_refs, layer
):
    node_rows(layer, own_ref, part_ref, other_ref, nodes_ref, first_ref, second_ref, new_ref)
    for i, out_ref in enumerate(out_refs):
        send_rows(side_ref[0], rows_ref, 2 * i, new_ref, out_ref, 0)


def node_probe_kernel(
    side_ref,
    rows_ref,
    far_rows_ref,
    own_ref,
    part_ref,
    other_ref,
    nodes_ref,
    first_ref,
    second_ref,
    new_ref,
    *out_refs,
    layer,
):
    node_rows(layer, own_ref, part_ref, other_ref, nodes_ref, first_ref, second_ref, new_ref)
    slot = rows_ref.shape[1]
    for i, out_ref in enumerate(out_refs):
        send_rows(side_ref[0], rows_ref, 2 * i, new_ref, out_ref, 0)
        send_rows(side_ref[0], far_rows_ref, 2 * i, new_ref, out_ref, slot)


def weights_kernel(side_ref, slots_ref, wgt_ref, out_ref, *, slot):
    side = side_ref[0]
    half = out_ref.shape[1] // 2
    lane = lax.broadcasted_iota(jnp.int32, (LANES, LANES), 1)
    for start in range(0, out_ref.shape[0], LANES):
        places = []
        shares = []
        for k in range(slots_ref.shape[0]):
            pick = columns_of(slots_ref[pl.ds(k, 1), start : start + LANES])
            block = pick // slot
            place = (block // 2) * slot + pick % slot
            places.append(jnp.where(block % 2 == side, place, place + half))
            shares.append(columns_of(wgt_ref[pl.ds(k, 1), start : start + LANES]))
        for first in range(0, 2 * half, LANES):
            total = jnp.zeros((LANES, LANES), F32)
            for place, share in zip(places, shares):
                total += jnp.where(place == lane + first, share, 0.0)
            out_ref[start : start + LANES, first : first + LANES] = total.astype(BF16)


def decode_kernel(table_ref, embed_ref, first_ref, second_ref, a_ref, b_ref, c_ref, d_ref, other_ref, out_ref):
    slot = a_ref.shape[0] // 2
    half = 4 * slot
    interp = dot(table_ref[:, half:], other_ref[...])
    for i, ref in enumerate((a_ref, b_ref, c_ref, d_ref)):
        interp += dot(table_ref[:, i * slot : (i + 1) * slot], ref[0:slot, :])
    decoder_in = (interp + embed_ref[...].astype(F32)).astype(BF16)
    hidden = jnp.maximum(dot(decoder_in, first_ref[...]), 0.0).astype(BF16)
    out_ref[...] = lax.dot_general(
        second_ref[...], hidden, (((1,), (1,)), ((), ())), preferred_element_type=F32
    )


SCALAR = pl.BlockSpec(memory_space=pltpu.SMEM)
ON_CHIP = pl.BlockSpec(memory_space=pltpu.VMEM)


def run(kernel, flops, outs, args, scratch=()):
    nbytes = sum(a.size * a.dtype.itemsize for a in args)
    return pl.pallas_call(
        kernel,
        in_specs=[SCALAR if a.ndim == 1 else ON_CHIP for a in args],
        out_specs=[ON_CHIP] * len(outs),
        out_shape=[jax.ShapeDtypeStruct(shape, dtype) for shape, dtype in outs],
        scratch_shapes=list(scratch),
        compiler_params=pltpu.CompilerParams(vmem_limit_bytes=VMEM_GRANT),
        cost_estimate=pl.CostEstimate(flops=flops, bytes_accessed=nbytes, transcendentals=0),
    )(*args)


def exchanged(pieces, steps):
    got = []
    for piece, step in zip(pieces, steps):
        got.append(both_ways(piece, step))
    return got


def one_layer(layer, last, side, h, e, sends, src, dst, halo_rows, probe_rows, far_rows, weights):
    edge_first, edge_second, node_first, node_second = weights
    steps = steps_of_pairs(SPAN)
    pairs = len(steps)
    nodes, width = h.shape
    edges = e.shape[0]
    slot = halo_rows.shape[1]
    half = pairs * slot
    kept = jnp.concatenate(exchanged(sends, steps), axis=0)
    near, recv = run(
        functools.partial(edge_near_kernel, layer=layer),
        4 * nodes * width * width + 3 * edges * nodes * width,
        [((edges, width), F32), ((nodes, width), BF16)],
        (src, dst, h, edge_first),
        [pltpu.VMEM((nodes, width), BF16)],
    )
    other = swapped(kept)
    (mid,) = run(
        functools.partial(edge_kept_kernel, layer=layer, slot=slot),
        2 * width * (half * (width + edges) + edges * width) + edges * nodes * width,
        [((edges, width), F32)],
        (side, src, dst, e, recv, kept, edge_first),
        [pltpu.VMEM((half, width), BF16)],
    )
    e, part = run(
        functools.partial(edge_post_kernel, layer=layer, slot=slot),
        2 * width * (half * (width + edges) + edges * (width + nodes)),
        [((edges, width), BF16), ((nodes, width), BF16)],
        (side, src, dst, near, mid, e, other, edge_first, edge_second),
        [pltpu.VMEM((half, width), BF16)],
    )
    part_other = swapped(part)
    (own,) = run(
        functools.partial(node_own_kernel, layer=layer),
        2 * nodes * width * width,
        [((nodes, width), F32)],
        (h, node_first),
    )
    node_args = (own, part, part_other, h, node_first, node_second)
    node_flops = 4 * nodes * width * width
    if not last:
        h, *sends = run(
            functools.partial(node_kernel, layer=layer),
            node_flops + 2 * half * nodes * width,
            [((nodes, width), BF16)] + [((slot, width), BF16)] * pairs,
            (side, halo_rows) + node_args,
        )
    else:
        qslot = probe_rows.shape[1]
        h, *sends = run(
            functools.partial(node_probe_kernel, layer=layer),
            node_flops + 4 * pairs * qslot * nodes * width,
            [((nodes, width), BF16)] + [((2 * qslot, width), BF16)] * pairs,
            (side, probe_rows, far_rows) + node_args,
        )
    return h, e, sends


def body(
    node_lat,
    edge_lat,
    edge_src,
    edge_dst,
    halo_rows,
    probe_rows,
    probe_slot,
    probe_wgt,
    probe_embed,
    edge_first,
    edge_second,
    node_first,
    node_second,
    decode_first,
    decode_second,
):
    steps = steps_of_pairs(SPAN)
    pairs = len(steps)
    side = lax.axis_index("feat").astype(jnp.int32).reshape(1)
    nodes, width = node_lat.shape
    edges = edge_lat.shape[0]
    slot = halo_rows.shape[1]
    qslot = probe_rows.shape[1]
    probes = probe_slot.shape[0]
    layers = edge_first.shape[0]
    src = edge_src.reshape(edges // LANES, LANES)
    dst = edge_dst.reshape(edges // LANES, LANES)
    weights = (edge_first, edge_second, node_first, node_second)
    h = node_lat
    e = edge_lat
    sends = run(
        halo_send_kernel,
        2 * pairs * slot * nodes * width,
        [((slot, width), BF16)] * pairs,
        (side, halo_rows, h),
    )
    far_rows = swapped(probe_rows)
    for layer in range(layers):
        h, e, sends = one_layer(
            layer, layer + 1 == layers, side, h, e, sends, src, dst, halo_rows, probe_rows, far_rows, weights
        )
    got = exchanged(sends, steps)
    slots_t = probe_slot.T
    wgt_t = probe_wgt.T
    (table,) = run(
        functools.partial(weights_kernel, slot=qslot),
        8 * probes * pairs * 2 * qslot * pairs * 2,
        [((probes, 2 * pairs * qslot), BF16)],
        (side, slots_t, wgt_t),
    )
    other = swapped(jnp.concatenate([piece[qslot:] for piece in got], axis=0))
    (fields,) = run(
        decode_kernel,
        2 * probes * width * (2 * pairs * qslot + width),
        [((decode_second.shape[0], probes), F32)],
        (table, probe_embed, decode_first, decode_second, *got, other),
    )
    return (h, fields)


def solution(mesh):
    return jax.shard_map(
        body,
        mesh=mesh,
        in_specs=(
            P("dom", None),
            P(("dom", "feat"), None),
            P(("dom", "feat")),
            P(("dom", "feat")),
            P("dom", None),
            P(("dom", "feat"), None),
            P(("dom", "feat"), None),
            P(("dom", "feat"), None),
            P(("dom", "feat"), None),
            P(),
            P(),
            P(),
            P(),
            P(),
            P(),
        ),
        out_specs=(P("dom", None), P(None, ("dom", "feat"))),
        check_vma=False,
    )
```

```python
import functools

import jax
import jax.numpy as jnp
from jax import lax
from jax.experimental import pallas as pl
from jax.experimental.pallas import tpu as pltpu
from jax.sharding import PartitionSpec as P

SPAN = 4
LANES = 128
CHUNK = 256
VMEM_GRANT = 24 << 20
HALO_ORDER = [2, 0, 3, 1]
PROBE_ORDER = [2, 3, 1, 0]
DIRECT = [0, 1]
SPLIT = [2, 3]
EARLY_FLOPS = 10**10
BF16 = jnp.bfloat16
F32 = jnp.float32


def offset_pairs(width):
    return [1, width, width + 1, width - 1]


def both_ways(value, steps):
    count = lax.axis_size("dom")
    pairs = []
    for source in range(count):
        pairs.append((2 * source, 2 * ((source + steps) % count)))
        pairs.append((2 * source + 1, 2 * ((source - steps) % count) + 1))
    return lax.ppermute(value, ("dom", "feat"), pairs)


def passed_along(value, steps):
    count = lax.axis_size("dom")
    return lax.ppermute(value, "dom", [(source, (source + steps) % count) for source in range(count)])


def swapped(value):
    return lax.ppermute(value, "feat", [(0, 1), (1, 0)])


def dot(left, right):
    return jnp.dot(left, right, preferred_element_type=F32)


def normed(values):
    shifted = values - jnp.mean(values, axis=-1, keepdims=True)
    spread = jnp.mean(shifted * shifted, axis=-1, keepdims=True)
    return shifted * lax.rsqrt(spread + 1e-05)


def columns_of(row):
    return jnp.broadcast_to(row, (LANES, row.shape[1])).T


def picks(columns, base, width):
    lane = lax.broadcasted_iota(jnp.int32, columns.shape, 1)
    parts = []
    for start in range(0, width, LANES):
        parts.append(jnp.where(columns == lane + (base + start), 1.0, 0.0).astype(BF16))
    return jnp.concatenate(parts, axis=1)


def index_columns(rows, first, count):
    per = rows.shape[1]
    parts = [columns_of(rows[r : r + 1, :]) for r in range(first // per, (first + count) // per)]
    return jnp.concatenate(parts, axis=0) if len(parts) > 1 else parts[0]


def chosen_rows(side, lists_ref, pair):
    even = lists_ref[pl.ds(2 * pair, 1), :]
    odd = lists_ref[pl.ds(2 * pair + 1, 1), :]
    return jnp.where(side == 0, even, odd)


def first_kernel(out_ref):
    out_ref[...] = jnp.zeros(out_ref.shape, out_ref.dtype)


def plan_kernel(rows_ref, far_rows_ref, plan_ref):
    side = lax.axis_index("feat")
    for pair in DIRECT:
        plan_ref[2 * pair : 2 * pair + 2, :] = rows_ref[2 * pair : 2 * pair + 2, :]
    for pair in SPLIT:
        plan_ref[2 * pair : 2 * pair + 1, :] = chosen_rows(side, rows_ref, pair)
        plan_ref[2 * pair + 1 : 2 * pair + 2, :] = chosen_rows(side, far_rows_ref, pair)


def halo_send_kernel(ready_ref, rows_ref, nodes_ref, *out_refs):
    for i, out_ref in enumerate(out_refs):
        row = chosen_rows(lax.axis_index("feat"), rows_ref, i)
        select = picks(columns_of(row), 0, nodes_ref.shape[0])
        out_ref[...] = dot(select, nodes_ref[...]).astype(BF16)


def edge_near_kernel(src_ref, dst_ref, nodes_ref, first_ref, near_ref, recv_ref, own_ref, *, layer):
    count, width = nodes_ref.shape
    own_ref[...] = dot(nodes_ref[...], first_ref[layer, width : 2 * width, :]).astype(BF16)
    recv_ref[...] = dot(nodes_ref[...], first_ref[layer, 2 * width : 3 * width, :]).astype(BF16)
    total_edges = near_ref.shape[0]
    src, dst = src_ref[...], dst_ref[...]
    for start in range(0, total_edges, CHUNK):
        total = dot(picks(index_columns(src, start, CHUNK), 0, count), own_ref[...])
        if start < total_edges // 2:
            total += dot(picks(index_columns(dst, start, CHUNK), 0, count), recv_ref[...])
        near_ref[start : start + CHUNK, :] = total


def edge_self_kernel(edges_ref, first_ref, self_ref, *, layer):
    self_ref[...] = dot(edges_ref[...], first_ref[layer, 0 : edges_ref.shape[1], :])


def halo_places(far, slot, side):
    block = lax.div(far, slot)
    place = lax.div(block, 2) * slot + lax.rem(far, slot)
    kept = lax.rem(block, 2) == side
    inside = far >= 0
    mine = jnp.where(jnp.logical_and(inside, kept), place, -1)
    others = jnp.where(jnp.logical_and(inside, jnp.logical_not(kept)), place, -1)
    return mine, others


def edge_kept_kernel(
    src_ref, dst_ref, self_ref, recv_ref, kept_ref, first_ref, mid_ref, table_ref, *, layer, slot
):
    side = lax.axis_index("feat")
    half, width = kept_ref.shape
    count = recv_ref.shape[0]
    total_edges = self_ref.shape[0]
    table_ref[...] = dot(kept_ref[...], first_ref[layer, width : 2 * width, :]).astype(BF16)
    mine, _ = halo_places(src_ref[...] - count, slot, side)
    dst = dst_ref[...]
    for start in range(0, total_edges, CHUNK):
        span = slice(start, start + CHUNK)
        total = self_ref[span, :] + dot(picks(index_columns(mine, start, CHUNK), 0, half), table_ref[...])
        if start >= total_edges // 2:
            total += dot(picks(index_columns(dst, start, CHUNK), 0, count), recv_ref[...])
        mid_ref[span, :] = total


def summed_rows(dst_ref, new_ref, out_ref, base):
    total_edges = new_ref.shape[0]
    for start in range(0, out_ref.shape[0], CHUNK):
        node = lax.broadcasted_iota(jnp.int32, (CHUNK, LANES), 0) + (base + start)
        parts = []
        for r in range(total_edges // LANES):
            row = jnp.broadcast_to(dst_ref[pl.ds(r, 1), :], (CHUNK, LANES))
            parts.append(jnp.where(row == node, 1.0, 0.0).astype(BF16))
        out_ref[start : start + CHUNK, :] = dot(jnp.concatenate(parts, axis=1), new_ref[...]).astype(BF16)


def edge_new_kernel(
    src_ref,
    dst_ref,
    near_ref,
    mid_ref,
    edges_ref,
    other_ref,
    first_ref,
    second_ref,
    new_ref,
    part_ref,
    table_ref,
    *,
    layer,
    slot,
    count,
):
    side = lax.axis_index("feat")
    half, width = other_ref.shape
    total_edges = edges_ref.shape[0]
    table_ref[...] = dot(other_ref[...], first_ref[layer, width : 2 * width, :]).astype(BF16)
    _, others = halo_places(src_ref[...] - count, slot, side)
    for start in range(0, total_edges, CHUNK):
        span = slice(start, start + CHUNK)
        hidden = near_ref[span, :] + mid_ref[span, :]
        hidden += dot(picks(index_columns(others, start, CHUNK), 0, half), table_ref[...])
        hidden = jnp.maximum(hidden, 0.0).astype(BF16)
        update = normed(dot(hidden, second_ref[layer]))
        new_ref[span, :] = (edges_ref[span, :].astype(F32) + update).astype(BF16)
    summed_rows(dst_ref, new_ref, part_ref, 0)


def edge_rest_kernel(dst_ref, new_ref, part_ref):
    summed_rows(dst_ref, new_ref, part_ref, part_ref.shape[0])


def node_own_kernel(rows_ref, nodes_ref, first_ref, own_ref, rows_own_ref, rows_nodes_ref, *, layer, direct):
    count, width = nodes_ref.shape
    top = first_ref[layer, 0:width, :]
    own_ref[...] = dot(nodes_ref[...], top)
    for i, columns in enumerate(send_columns(rows_ref, direct)):
        size = columns.shape[0]
        picked = dot(picks(columns, 0, count), nodes_ref[...]).astype(BF16)
        rows_nodes_ref[i * size : (i + 1) * size, :] = picked
    rows_own_ref[...] = dot(rows_nodes_ref[...], top)


def send_columns(rows_ref, direct):
    if direct is None:
        return [columns_of(chosen_rows(lax.axis_index("feat"), rows_ref, i)) for i in range(rows_ref.shape[0] // 2)]
    return [columns_of(rows_ref[pl.ds(k, 1), :]) for k in direct]


def node_update(nodes, own, summed, bottom, second):
    hidden = jnp.maximum(own + dot(summed, bottom), 0.0).astype(BF16)
    return (nodes.astype(F32) + normed(dot(hidden, second))).astype(BF16)


def node_send_kernel(
    rows_ref,
    part_a_ref,
    part_b_ref,
    other_a_ref,
    other_b_ref,
    rows_own_ref,
    rows_nodes_ref,
    first_ref,
    second_ref,
    summed_ref,
    *out_refs,
    layer,
    direct,
):
    count, width = summed_ref.shape
    half = count // 2
    summed_ref[0:half, :] = (part_a_ref[...].astype(F32) + other_a_ref[...].astype(F32)).astype(BF16)
    summed_ref[half:count, :] = (part_b_ref[...].astype(F32) + other_b_ref[...].astype(F32)).astype(BF16)
    bottom = first_ref[layer, width : 2 * width, :]
    second = second_ref[layer]
    columns = send_columns(rows_ref, direct)
    picked = jnp.concatenate([picks(c, 0, count) for c in columns], axis=0)
    picked = dot(picked, summed_ref[...]).astype(BF16)
    fresh = node_update(rows_nodes_ref[...], rows_own_ref[...], picked, bottom, second)
    for i, out_ref in enumerate(out_refs):
        size = out_ref.shape[0]
        out_ref[...] = fresh[i * size : (i + 1) * size, :]


def node_full_kernel(rows_ref, own_ref, summed_ref, nodes_ref, first_ref, second_ref, new_ref, *out_refs, layer, lists):
    count, width = nodes_ref.shape
    bottom = first_ref[layer, width : 2 * width, :]
    second = second_ref[layer]
    for start in range(0, count, CHUNK):
        span = slice(start, start + CHUNK)
        new_ref[span, :] = node_update(nodes_ref[span, :], own_ref[span, :], summed_ref[span, :], bottom, second)
    for picked, out_ref in zip(lists, out_refs):
        select = jnp.concatenate([picks(columns_of(rows_ref[pl.ds(k, 1), :]), 0, count) for k in picked], axis=0)
        out_ref[...] = dot(select, new_ref[...]).astype(BF16)


def weights_kernel(slots_ref, wgt_ref, out_ref, *, slot):
    side = lax.axis_index("feat")
    lane = lax.broadcasted_iota(jnp.int32, (LANES, LANES), 1)
    block = lax.div(slots_ref[...], slot)
    turn = lax.rem(block, 2)
    spot = jnp.zeros_like(block)
    for i, pair in enumerate(SPLIT):
        spot = jnp.where(lax.div(block, 2) == pair, jnp.where(turn == side, i, len(SPLIT) + i), spot)
    for i, pair in enumerate(DIRECT):
        spot = jnp.where(lax.div(block, 2) == pair, 2 * len(SPLIT) + 2 * i + turn, spot)
    spot = spot * slot + lax.rem(slots_ref[...], slot)
    for start in range(0, out_ref.shape[0], LANES):
        places = [columns_of(spot[k : k + 1, start : start + LANES]) for k in range(slots_ref.shape[0])]
        shares = [columns_of(wgt_ref[pl.ds(k, 1), start : start + LANES]) for k in range(slots_ref.shape[0])]
        for first in range(0, out_ref.shape[1], LANES):
            total = jnp.zeros((LANES, LANES), F32)
            for place, share in zip(places, shares):
                total += jnp.where(place == lane + first, share, 0.0)
            out_ref[start : start + LANES, first : first + LANES] = total.astype(BF16)


def interp_kernel(table_ref, embed_ref, *rest):
    *got_refs, out_ref = rest
    slot = table_ref.shape[1] // (2 * len(SPLIT) + 2 * len(DIRECT))
    total = embed_ref[...].astype(F32)
    for i, ref in enumerate(got_refs):
        at = i * slot if i < len(SPLIT) else (len(SPLIT) + i) * slot
        total += dot(table_ref[:, at : at + slot], ref[0:slot, :])
    out_ref[...] = total


def decode_kernel(table_ref, total_ref, other_ref, first_ref, second_ref, out_ref):
    half = other_ref.shape[0]
    total = total_ref[...] + dot(table_ref[:, half : 2 * half], other_ref[...])
    hidden = jnp.maximum(dot(total.astype(BF16), first_ref[...]), 0.0).astype(BF16)
    out_ref[...] = lax.dot_general(
        second_ref[...], hidden, (((1,), (1,)), ((), ())), preferred_element_type=F32
    )


SCALAR = pl.BlockSpec(memory_space=pltpu.SMEM)
ON_CHIP = pl.BlockSpec(memory_space=pltpu.VMEM)


def run(kernel, flops, outs, args, scratch=()):
    nbytes = sum(a.size * a.dtype.itemsize for a in args)
    return pl.pallas_call(
        kernel,
        in_specs=[SCALAR if a.ndim == 1 else ON_CHIP for a in args],
        out_specs=[SCALAR if len(shape) == 1 else ON_CHIP for shape, _ in outs],
        out_shape=[jax.ShapeDtypeStruct(shape, dtype) for shape, dtype in outs],
        scratch_shapes=list(scratch),
        compiler_params=pltpu.CompilerParams(vmem_limit_bytes=VMEM_GRANT),
        cost_estimate=pl.CostEstimate(flops=flops, bytes_accessed=nbytes, transcendentals=0),
    )(*args)


def body(
    node_lat,
    edge_lat,
    edge_src,
    edge_dst,
    halo_rows,
    probe_rows,
    probe_slot,
    probe_wgt,
    probe_embed,
    edge_first,
    edge_second,
    node_first,
    node_second,
    decode_first,
    decode_second,
):
    steps = offset_pairs(SPAN)
    pairs = len(steps)
    nodes, width = node_lat.shape
    edges = edge_lat.shape[0]
    slot = halo_rows.shape[1]
    qslot = probe_rows.shape[1]
    probes = probe_slot.shape[0]
    layers = edge_first.shape[0]
    half = pairs * slot
    square = 2 * width * width
    e = edge_lat
    h = node_lat
    src = edge_src.reshape(edges // LANES, LANES)
    dst = edge_dst.reshape(edges // LANES, LANES)
    (ready,) = run(first_kernel, EARLY_FLOPS, [((8, LANES), F32)], ())
    sends = run(halo_send_kernel, EARLY_FLOPS, [((slot, width), BF16)] * pairs, (ready, halo_rows, h))
    far_rows = swapped(probe_rows)
    node_full = None
    for layer in range(layers):
        last = layer + 1 == layers
        got = {}
        for i in HALO_ORDER:
            got[i] = both_ways(sends[i], steps[i])
        kept = jnp.concatenate([got[i] for i in range(pairs)], axis=0)
        if layer > 0:
            (h,) = node_full()
        near, recv = run(
            functools.partial(edge_near_kernel, layer=layer),
            2 * square * nodes + 3 * edges * nodes * width,
            [((edges, width), F32), ((nodes, width), BF16)],
            (src, dst, h, edge_first),
            [pltpu.VMEM((nodes, width), BF16)],
        )
        (self_part,) = run(
            functools.partial(edge_self_kernel, layer=layer), square * edges, [((edges, width), F32)], (e, edge_first)
        )
        if layer == 0:
            (plan,) = run(plan_kernel, 1000, [(probe_rows.shape, jnp.int32)], (probe_rows, far_rows))
        other = swapped(kept)
        (mid,) = run(
            functools.partial(edge_kept_kernel, layer=layer, slot=slot),
            square * half + 2 * half * edges * width + edges * nodes * width,
            [((edges, width), F32)],
            (src, dst, self_part, recv, kept, edge_first),
            [pltpu.VMEM((half, width), BF16)],
        )
        e, part_a = run(
            functools.partial(edge_new_kernel, layer=layer, slot=slot, count=nodes),
            square * (half + edges) + width * edges * (2 * half + nodes),
            [((edges, width), BF16), ((nodes // 2, width), BF16)],
            (src, dst, near, mid, e, other, edge_first, edge_second),
            [pltpu.VMEM((half, width), BF16)],
        )
        other_a = swapped(part_a)
        (part_b,) = run(edge_rest_kernel, width * edges * nodes, [((nodes // 2, width), BF16)], (dst, e))
        other_b = swapped(part_b)
        lists = plan if last else halo_rows
        direct = [2 * PROBE_ORDER[0], 2 * PROBE_ORDER[0] + 1] if last else None
        size = lists.shape[1]
        rows = 2 * size if last else half
        piece = rows if last and PROBE_ORDER[0] in SPLIT else size
        own, rows_own, rows_nodes = run(
            functools.partial(node_own_kernel, layer=layer, direct=direct),
            square * (nodes + rows) + 2 * rows * nodes * width,
            [((nodes, width), F32), ((rows, width), F32), ((rows, width), BF16)],
            (lists, h, node_first),
        )
        summed, *sends = run(
            functools.partial(node_send_kernel, layer=layer, direct=direct),
            2 * square * rows + 2 * rows * nodes * width,
            [((nodes, width), BF16)] + [((piece, width), BF16)] * (rows // piece),
            (lists, part_a, part_b, other_a, other_b, rows_own, rows_nodes, node_first, node_second),
        )
        picked = []
        for i in PROBE_ORDER[1:] if last else []:
            picked += [[2 * i], [2 * i + 1]] if i in DIRECT else [[2 * i, 2 * i + 1]]
        node_full = functools.partial(
            run,
            functools.partial(node_full_kernel, layer=layer, lists=picked),
            2 * square * nodes + 2 * sum(map(len, picked)) * size * nodes * width,
            [((nodes, width), BF16)] + [((len(p) * size, width), BF16) for p in picked],
            (lists, own, summed, h, node_first, node_second),
        )
    h, *rest = node_full()
    pieces = iter(list(sends) + rest)
    got = {}
    for i in PROBE_ORDER:
        for turn in range(2 if i in DIRECT else 1):
            if i in DIRECT:
                got[2 * i + turn] = passed_along(next(pieces), steps[i] * (1 - 2 * turn))
            else:
                got[2 * i] = both_ways(next(pieces), steps[i])
    kept = [got[2 * i] for i in SPLIT]
    ends = [got[2 * i + turn] for i in DIRECT for turn in range(2)]
    (table,) = run(
        functools.partial(weights_kernel, slot=qslot),
        48 * probes * pairs * qslot * pairs,
        [((probes, 2 * pairs * qslot), BF16)],
        (probe_slot.T, probe_wgt.T),
    )
    other = swapped(jnp.concatenate([piece[qslot:] for piece in kept], axis=0))
    (total,) = run(
        interp_kernel,
        2 * probes * width * (len(kept) + len(ends)) * qslot,
        [((probes, width), F32)],
        (table, probe_embed, *kept, *ends),
    )
    (fields,) = run(
        decode_kernel,
        2 * probes * width * (len(kept) * qslot + width),
        [((decode_second.shape[0], probes), F32)],
        (table, total, other, decode_first, decode_second),
    )
    return (h, fields)


def solution(mesh):
    return jax.shard_map(
        body,
        mesh=mesh,
        in_specs=(
            P("dom", None),
            P(("dom", "feat"), None),
            P(("dom", "feat")),
            P(("dom", "feat")),
            P("dom", None),
            P(("dom", "feat"), None),
            P(("dom", "feat"), None),
            P(("dom", "feat"), None),
            P(("dom", "feat"), None),
            P(),
            P(),
            P(),
            P(),
            P(),
            P(),
        ),
        out_specs=(P("dom", None), P(None, ("dom", "feat"))),
        check_vma=False,
    )
```
